256 devices in a mesh: batch: 4 (over x_hi, core), hidden: 16 (over x_lo, z), width: 4 (over y).
Axes of the slice: x: 4 (x_hi: 2, x_lo: 2; x = x_hi * 2 + x_lo), y: 4, z: 8, core: 2. Of those that a mesh axis runs over, the one named last changes fastest.
Arguments:
- frames: bfloat16 [4, 512, 1280], P('batch', None, 'hidden'), may hold values from -6 to 6
- adapter_weight: bfloat16 [4, 1280, 16384], P(None, 'hidden', 'width'), may hold values from -0.078125 to 0.078125
- text_embed: bfloat16 [512, 16384], P('batch', 'width'), may hold values from -6 to 6
- audio_len: int32 [4], P('batch'), may hold values from 16 to 64, as said below
- text_len: int32 [4], P('batch'), may hold values from 32 to 112, as said below
- norm_gain: bfloat16 [16384], P('width'), may hold values from 0.5 to 1.5
- gate_up: bfloat16 [16384, 2, 26624], P('width', None, ('batch', 'hidden')), may hold values from -0.046875 to 0.046875
- cotangent: bfloat16 [512, 26624], P('width', ('batch', 'hidden')), may hold values from -0.59765625 to 0.59765625
Outputs:
- hidden: bfloat16 [512, 26624], P('width', ('batch', 'hidden'))
- weight_grad: float32 [4, 1280, 16384], P(None, 'hidden', 'width')
The draws below stay inside these ranges and needn't reach their ends.
Inputs may be any that keep to these rules, and one draw needn't show every extreme that they name: `audio_len`: some sequence holds exactly 16 audio positions and another exactly 64. audio_len + text_len never exceeds 128, and equals it in some sequence.
All inputs are finite; a program needn't handle non-finite values.
Results may differ from the reference program's by a relative error of at most 0.0059.
Values may be sent and summed in bfloat16 or wider, within the bound.
A program may use at most 64 MiB of HBM per device.

```python
import jax
import jax.numpy as jnp
from jax import lax

D = 16384
FF = 26624
FEAT = 1280
LEN = 128
ROWS = 4
TOKENS = 512


def length_pair(key):
    folded = jax.random.fold_in(key, 7)
    subkeys = jax.random.split(folded, 3)
    row_ids = jnp.arange(ROWS, dtype=jnp.int32)
    order = jax.random.permutation(subkeys[0], ROWS).astype(jnp.int32)
    short_row = order[0]
    long_row = order[1]
    audio_count = jax.random.randint(subkeys[1], (ROWS,), LEN // 8, LEN // 2 + 1)
    audio_count = jnp.where(row_ids == short_row, LEN // 2, audio_count)
    audio_count = jnp.where(row_ids == long_row, LEN // 8, audio_count)
    pad_count = jax.random.randint(subkeys[2], (ROWS,), 0, LEN // 4 + 1)
    pad_count = jnp.where(row_ids == short_row, LEN // 4, pad_count)
    pad_count = jnp.where(row_ids == long_row, 0, pad_count)
    return (audio_count.astype(jnp.int32), (LEN - audio_count - pad_count).astype(jnp.int32))


def draw_audio_len(key, part):
    return length_pair(key)[0]


def draw_text_len(key, part):
    return length_pair(key)[1]


def levels(own_key, dims, cuts, least, high):
    def one(axis_at, blocks):
        steps = jax.random.uniform(jax.random.fold_in(jax.random.fold_in(own_key, 6), axis_at), (blocks,), jnp.float32, least / len(cuts), high / len(cuts))
        return jnp.repeat(jnp.exp(steps), dims[axis_at] // blocks).reshape((-1,) + (1,) * (len(dims) - axis_at - 1))

    gain = one(*cuts[0])
    for cut in cuts[1:]:
        gain = gain * one(*cut)
    return gain


def normal_values(stream_key, extent, scale, limit, cuts=(), kind=jnp.bfloat16):
    drawn = scale * jax.random.normal(stream_key, extent, jnp.float32)
    if cuts:
        drawn = drawn * levels(stream_key, extent, cuts, -0.22, 0.18)
    return jnp.clip(drawn, -limit, limit).astype(kind)


def setup_inputs(seed: int = 0) -> dict:
    splits = jax.random.split(jax.random.key(seed), 9)
    frames = normal_values(splits[0], (ROWS, 4 * LEN, FEAT), 1.0, 6.0, ((0, 4), (2, 16)))
    adapter_weight = normal_values(splits[1], (4, FEAT, D), (4 * FEAT) ** -0.5, 0.078125, ((1, 16), (2, 4)))
    text_embed = normal_values(splits[2], (TOKENS, D), 1.0, 6.0, ((0, 4), (1, 4)))
    audio_len = draw_audio_len(jax.random.fold_in(splits[8], 71), 0)
    text_len = draw_text_len(jax.random.fold_in(splits[8], 71), 0)
    norm_gain = jnp.clip(1.0 + 0.1 * jax.random.normal(splits[5], (D,), jnp.float32), 0.5, 1.5).astype(jnp.bfloat16)
    gate_up = normal_values(splits[6], (D, 2, FF), D ** -0.5, 0.046875, ((0, 4), (2, 64)))
    cotangent = normal_values(splits[7], (TOKENS, FF), 0.1, 0.59765625, ((0, 4), (1, 64)))
    return {"frames": frames, "adapter_weight": adapter_weight, "text_embed": text_embed, "audio_len": audio_len, "text_len": text_len, "norm_gain": norm_gain, "gate_up": gate_up, "cotangent": cotangent}


norm_eps = 1e-05

def reference(frames, adapter_weight, text_embed, audio_len, text_len, norm_gain, gate_up, cotangent):
    stacked = frames.reshape(TOKENS, 4 * FEAT)
    kernel = adapter_weight.reshape(4 * FEAT, D)
    audio_part = jnp.dot(stacked, kernel, preferred_element_type=jnp.float32)
    token_ids = jnp.arange(TOKENS, dtype=jnp.int32)
    positions = token_ids % LEN
    row_index = token_ids // LEN
    audio_count = audio_len[row_index]
    text_count = text_len[row_index]
    is_audio = positions < audio_count
    is_text = jnp.logical_and(jnp.logical_not(is_audio), positions < audio_count + text_count)
    stream = jnp.where(is_audio[:, None], audio_part, jnp.where(is_text[:, None], text_embed.astype(jnp.float32), jnp.zeros_like(audio_part)))
    sum_squares = lax.optimization_barrier(jnp.sum(stream * stream, axis=1))
    inv_rms = lax.rsqrt(sum_squares / D + norm_eps)
    unit_stream = stream * inv_rms[:, None]
    gain_vals = norm_gain.astype(jnp.float32)
    normed = (unit_stream * gain_vals[None, :]).astype(jnp.bfloat16)
    weights = gate_up.reshape(D, 2 * FF)
    summed = jnp.dot(normed, weights, preferred_element_type=jnp.float32)
    gate_vals = summed[:, :FF]
    up_vals = summed[:, FF:]
    sigmoid_gate = jax.nn.sigmoid(gate_vals)
    silu_gate = gate_vals * sigmoid_gate
    hidden = (silu_gate * up_vals).astype(jnp.bfloat16)
    cot_vals = cotangent.astype(jnp.float32)
    silu_slope = sigmoid_gate * (1.0 + gate_vals * (1.0 - sigmoid_gate))
    grad_gate = (cot_vals * up_vals * silu_slope).astype(jnp.bfloat16)
    grad_up = (cot_vals * silu_gate).astype(jnp.bfloat16)
    grad_pair = jnp.concatenate([grad_gate, grad_up], axis=1)
    normed_grad = lax.dot_general(grad_pair, weights, (((1,), (1,)), ((), ())), preferred_element_type=jnp.float32)
    scaled_grad = normed_grad * gain_vals[None, :]
    proj_stat = lax.optimization_barrier(jnp.sum(unit_stream * scaled_grad, axis=1)) / D
    stream_grad = (scaled_grad - unit_stream * proj_stat[:, None]) * inv_rms[:, None]
    audio_grad = jnp.where(is_audio[:, None], stream_grad, jnp.zeros_like(stream_grad)).astype(jnp.bfloat16)
    weight_grad = lax.dot_general(stacked, audio_grad, (((0,), (0,)), ((), ())), preferred_element_type=jnp.float32)
    return (hidden, weight_grad.reshape(4, FEAT, D))
```

```python
import jax
import jax.numpy as jnp
from jax import lax
from jax.sharding import PartitionSpec as P

D = 16384
HEAD = 64
norm_eps = 1e-05


def on_device(
    frames, adapter_weight, text_embed, audio_len, text_len, norm_gain, gate_up, cotangent
):
    feat_here = frames.shape[2]
    seq_len = frames.shape[1] // 4
    width_here = adapter_weight.shape[2]
    stacked = frames[0, : 4 * HEAD].reshape(HEAD, 4 * feat_here)
    kernel = adapter_weight.reshape(4 * feat_here, width_here)
    partial_audio = jnp.dot(stacked, kernel, preferred_element_type=jnp.float32)
    audio_part = lax.psum(partial_audio, "hidden")
    positions = jnp.arange(seq_len, dtype=jnp.int32)
    is_audio = positions < audio_len[0]
    is_text = jnp.logical_and(jnp.logical_not(is_audio), positions < audio_len[0] + text_len[0])
    text_vals = jnp.where(is_text[:, None], text_embed.astype(jnp.float32), 0.0)
    stream = jnp.concatenate(
        [jnp.where(is_audio[:HEAD, None], audio_part, text_vals[:HEAD]), text_vals[HEAD:]], axis=0
    )
    gain_vals = norm_gain.astype(jnp.float32)
    sum_squares = lax.psum(jnp.sum(stream * stream, axis=1), "width")
    inv_rms = lax.rsqrt(sum_squares / D + norm_eps)
    normed = (stream * inv_rms[:, None] * gain_vals[None, :]).astype(jnp.bfloat16)
    masked = jnp.where(is_audio[:HEAD, None], stacked, jnp.zeros_like(stacked))
    all_stacked = lax.all_gather(masked, "batch", axis=0, tiled=True)
    all_inv = lax.all_gather(inv_rms[:HEAD], "batch", axis=0, tiled=True)
    all_normed = lax.all_gather(normed, "batch", axis=0, tiled=True)
    weights = gate_up.reshape(width_here, -1)
    half = weights.shape[1] // 2
    partial_pair = jnp.dot(all_normed, weights, preferred_element_type=jnp.float32)
    summed = lax.psum_scatter(partial_pair, "width", scatter_dimension=0, tiled=True)
    gate_vals = summed[:, :half]
    up_vals = summed[:, half:]
    sigmoid_gate = jax.nn.sigmoid(gate_vals)
    silu_gate = gate_vals * sigmoid_gate
    hidden = (silu_gate * up_vals).astype(jnp.bfloat16)
    cot_vals = cotangent[:HEAD].astype(jnp.float32)
    gate_head, up_head, sig_head = gate_vals[:HEAD], up_vals[:HEAD], sigmoid_gate[:HEAD]
    grad_gate = cot_vals * up_head * sig_head * (1.0 + gate_head * (1.0 - sig_head))
    grad_up = cot_vals * silu_gate[:HEAD]
    inner = jnp.sum(grad_gate * gate_head + grad_up * up_head, axis=1) / D
    grad_pair = jnp.concatenate([grad_gate, grad_up], axis=1).astype(jnp.bfloat16)
    all_pairs = lax.all_gather(grad_pair, "width", axis=0, tiled=True)
    all_inner = lax.all_gather(inner, "width", axis=0, tiled=True)
    partial = lax.dot_general(
        all_pairs, weights, (((1,), (1,)), ((), ())), preferred_element_type=jnp.float32
    )
    head_normed = all_normed.reshape(-1, seq_len, width_here)[:, :HEAD].reshape(-1, width_here)
    head_unit = head_normed.astype(jnp.float32) / gain_vals[None, :]
    share = (gain_vals[None, :] * partial - head_unit * all_inner[:, None]) * all_inv[:, None]
    grad_share = lax.psum_scatter(share, ("batch", "hidden"), scatter_dimension=0, tiled=True)
    audio_grad = lax.all_gather(
        grad_share.astype(jnp.bfloat16), ("batch", "hidden"), axis=0, tiled=True
    )
    weight_grad = lax.dot_general(
        all_stacked, audio_grad, (((0,), (0,)), ((), ())), preferred_element_type=jnp.float32
    )
    return (hidden, weight_grad.reshape(4, feat_here, width_here))


def solution(mesh):
    return jax.shard_map(
        on_device,
        mesh=mesh,
        in_specs=(
            P("batch", None, "hidden"),
            P(None, "hidden", "width"),
            P("batch", "width"),
            P("batch"),
            P("batch"),
            P("width"),
            P("width", None, ("batch", "hidden")),
            P("width", ("batch", "hidden")),
        ),
        out_specs=(P("width", ("batch", "hidden")), P(None, "hidden", "width")),
        check_vma=False,
    )
```

```python
import jax
import jax.numpy as jnp
from jax import lax
from jax.experimental import pallas as pl
from jax.experimental.pallas import tpu as pltpu
from jax.sharding import PartitionSpec as P

D = 16384
HEAD = 64
PADDED = 896
CHUNKS = 2
norm_eps = 1e-05
MESH = pl.DeviceIdType.MESH
BF = jnp.bfloat16
F32 = jnp.float32


def fused_kernel(
    alen, tlen, stacked, kernel, text, gains, cot, w_hbm,
    hidden_out, grad_out, frames_out,
    w, xh, xt, pa, sta, rxa, stz, rza, gst, gown, grx, gall, bst, brx, xst, xown, xrx, zst, zrx,
    send_sems, recv_sems, local_sem,
):
    batch, hid, y = (lax.axis_index(a) for a in ("batch", "hidden", "width"))
    xhi, c = batch // 2, batch % 2
    xlo, z = hid // 8, hid % 8
    x = xhi * 2 + xlo
    width = text.shape[1]
    units = w_hbm.shape[0]
    half = units // 2
    span = width // CHUNKS
    part = span // 8

    def device(x_=x, c_=c, z_=z, y_=y):
        return {"batch": (x_ // 2) * 2 + c_, "hidden": (x_ % 2) * 8 + z_, "width": y_}

    def zmod(k):
        return lax.rem(z + k, 8)

    def xmod(k):
        return lax.rem(x + k, 4)

    def ymod(k):
        return lax.rem(y + k, 4)

    def slot(seq):
        return (seq % 2) * 2 + seq // 2

    sibling = device(c_=1 - c)
    pair = device(x_=xhi * 2 + 1 - xlo)
    cross = device(x_=(1 - xhi) * 2 + 1 - xlo)
    z_peers = [device(z_=zmod(k)) for k in range(1, 8)]
    x_peers = [device(x_=xmod(k)) for k in range(1, 4)]
    y_peers = [device(y_=ymod(k)) for k in range(1, 4)]

    barrier = pltpu.get_barrier_semaphore()
    peers = [sibling] + z_peers + x_peers + y_peers
    for p in peers:
        pl.semaphore_signal(barrier, inc=1, device_id=p, device_id_type=MESH)

    started = []

    def send(src, dst, peer):
        i = len(started)
        copy = pltpu.make_async_remote_copy(
            src_ref=src, dst_ref=dst, send_sem=send_sems.at[i], recv_sem=recv_sems.at[i],
            device_id=peer, device_id_type=MESH,
        )
        copy.start()
        started.append(copy)
        return copy

    w_copy = pltpu.make_async_copy(w_hbm, w.at[pl.ds(0, units)], local_sem)
    w_copy.start()

    def rows(start, size):
        return pl.ds(pl.multiple_of(start, size), size)

    def tiles(count, body):
        def step(i, carry):
            body(i)
            return carry

        lax.fori_loop(0, count, step, 0)

    def audio_tile(i):
        lanes = pl.ds(pl.multiple_of(i * 512, 512), 512)
        pa[:, lanes] = jnp.dot(stacked[...], kernel[:, lanes], preferred_element_type=F32)

    tiles(width // 512, audio_tile)
    sta[...] = pa[rows(32 * (1 - xlo), 32), :].astype(BF)

    pl.semaphore_wait(barrier, len(peers))
    pair_copies = []
    for j in range(CHUNKS):
        lanes = pl.ds(j * span, span)
        pair_copies.append(send(sta.at[:, lanes], rxa.at[:, lanes], pair))

    audio_count = alen[0]
    filled = alen[0] + tlen[0]
    head_pos = lax.broadcasted_iota(jnp.int32, (HEAD, 1), 0)
    me = slot(batch)
    frames_out[rows(me * HEAD, HEAD), :] = jnp.where(
        head_pos < audio_count, stacked[...], jnp.zeros_like(stacked[...])
    )

    def tail_tile(i):
        lanes = pl.ds(pl.multiple_of(i * 512, 512), 512)
        vals = text[HEAD:, lanes].astype(F32)
        keep = jnp.where((head_pos + HEAD) < filled, vals, 0.0)
        xt[rows(me * HEAD, HEAD), lanes] = (keep * gains[0:1, lanes]).astype(BF)

    tiles(width // 512, tail_tile)
    mine = rows(me * HEAD, HEAD)
    theirs = rows(slot((1 - xhi) * 2 + c) * HEAD, HEAD)
    cross_copy = send(xt.at[mine], xt.at[mine], cross)
    tail_sib = send(xt.at[mine], xt.at[mine], sibling)
    f_far = send(frames_out.at[mine], frames_out.at[mine], device(x_=(1 - xhi) * 2 + xlo))
    f_sib = send(frames_out.at[mine], frames_out.at[mine], sibling)

    own_rows = rows(32 * xlo, 32)

    def piece(j, who):
        return pl.ds(pl.multiple_of(j * span + who * part, part), part)

    z_copies = []
    for j in range(CHUNKS):
        pair_copies[j].wait_recv()
        lanes = pl.ds(j * span, span)
        pa[own_rows, lanes] = pa[own_rows, lanes] + rxa[:, lanes].astype(F32)
        stz[:, lanes] = pa[own_rows, lanes].astype(BF)
        z_copies.append([
            send(stz.at[:, piece(j, zmod(k))], rza.at[k - 1, :, pl.ds(j * part, part)], z_peers[k - 1])
            for k in range(1, 8)
        ])

    place = rows(c * 128 + x * 32, 32)
    pos = lax.broadcasted_iota(jnp.int32, (32, 1), 0) + 32 * xlo

    def gather_z(buf, j):
        lanes = piece(j, z)
        return [send(buf.at[place, lanes], buf.at[place, lanes], p) for p in z_peers]

    def gather_x(buf, j):
        lanes = pl.ds(j * span, span)
        xs = [send(buf.at[place, lanes], buf.at[place, lanes], p) for p in x_peers]
        return xs, [send(buf.at[place, lanes], buf.at[place, lanes], sibling)]

    def forward(buf, j, xs, sibs):
        lanes = pl.ds(j * span, span)
        for k in range(1, 4):
            xs[k - 1].wait_recv()
            there = rows(c * 128 + xmod(4 - k) * 32, 32)
            sibs.append(send(buf.at[there, lanes], buf.at[there, lanes], sibling))

    ag = []
    for j in range(CHUNKS):
        lanes = piece(j, z)
        total = pa[own_rows, lanes]
        for k in range(7):
            z_copies[j][k].wait_recv()
            total = total + rza[k, :, pl.ds(j * part, part)].astype(F32)
        words = text[own_rows, lanes].astype(F32)
        stream = jnp.where(pos < audio_count, total, jnp.where(pos < filled, words, 0.0))
        xh[place, lanes] = (stream * gains[0:1, lanes]).astype(BF)
        ag.append(gather_z(xh, j))
    xcop = []
    for j in range(CHUNKS):
        for cp in ag[j]:
            cp.wait_recv()
        xcop.append(gather_x(xh, j))

    cross_copy.wait_recv()
    tail_fwd = send(xt.at[theirs], xt.at[theirs], sibling)
    f_far.wait_recv()
    f_fwd = send(frames_out.at[theirs], frames_out.at[theirs], sibling)
    w_copy.wait()
    w[pl.ds(units, PADDED - units), :] = jnp.zeros((PADDED - units, width), BF)
    tail_sib.wait_recv()
    tail_fwd.wait_recv()

    lane = lax.broadcasted_iota(jnp.int32, (256, 128), 1)
    mark = units - (PADDED - 128)

    def project(buf, dst):
        def square(i, acc):
            lanes = pl.ds(pl.multiple_of(i * 128, 128), 128)
            v = buf[:, lanes].astype(F32) * gains[1:2, lanes]
            return acc + v * v

        sq = lax.fori_loop(0, width // 128, square, jnp.zeros((256, 128), F32))
        sq = jnp.sum(sq, axis=1, keepdims=True)
        high = sq.astype(BF).astype(F32)
        low = sq - high
        for start in range(0, PADDED, 256):
            size = min(256, PADDED - start)
            out = lax.dot_general(
                buf[...], w[pl.ds(start, size), :], (((1,), (1,)), ((), ())),
                preferred_element_type=F32,
            )
            if start + size == PADDED:
                out = jnp.where(lane == mark, high, jnp.where(lane == mark + 1, low, out))
            dst[:, pl.ds(start, size)] = out.astype(BF)
        return [
            send(dst.at[rows(slot(ymod(k)) * HEAD, HEAD)], grx.at[yslot(dst, k)], y_peers[k - 1])
            for k in range(1, 4)
        ]

    def yslot(dst, k):
        return (0 if dst is gst else 3) + k - 1

    tail_y = project(xt, gst)

    for j in range(CHUNKS):
        forward(xh, j, *xcop[j])
    for j in range(CHUNKS):
        for cp in xcop[j][1]:
            cp.wait_recv()
    head_y = project(xh, gown)

    for cp in tail_y + head_y:
        cp.wait_recv()
    keep = rows(slot(y) * HEAD, HEAD)

    def total_of(own, base):
        t = own[keep, :].astype(F32)
        for k in range(3):
            t = t + grx[base + k].astype(F32)
        return t

    both = jnp.concatenate([total_of(gown, 3), total_of(gst, 0)], axis=0).T
    stat = both[units : units + 8]
    inv = lax.rsqrt((stat[0:1] + stat[1:2]) / D + norm_eps)
    gate = both[:half] * inv
    up = both[half:units] * inv
    sig = jax.nn.sigmoid(gate)
    silu = gate * sig
    hidden_out[...] = (silu * up).astype(BF)
    cotv = cot[...].astype(F32)
    g_gate = cotv * up * sig * (1.0 + gate * (1.0 - sig))
    g_up = cotv * silu
    inner = jnp.sum(g_gate * gate + g_up * up, axis=0, keepdims=True) * (inv * inv) / D
    high = inner.astype(BF).astype(F32)
    row = lax.broadcasted_iota(jnp.int32, (PADDED - units, 128), 0)
    extra = jnp.where(row == 0, high, jnp.where(row == 1, inner - high, 0.0))
    grads = jnp.concatenate([g_gate * inv, g_up * inv, extra], axis=0).T
    gall[keep, :] = grads[:HEAD].astype(BF)
    for cp in [send(gall.at[keep], gall.at[keep], p) for p in y_peers]:
        cp.wait_recv()

    lane128 = lax.broadcasted_iota(jnp.int32, (128, 128), 1)

    def share(base, i):
        block = rows(base, 128)
        lanes = pl.ds(pl.multiple_of(i * 512, 512), 512)
        last = gall[block, pl.ds(PADDED - 128, 128)].astype(F32)
        marked = jnp.logical_or(lane128 == mark, lane128 == mark + 1)
        coef = jnp.sum(jnp.where(marked, last, 0.0), axis=1, keepdims=True)
        out = jnp.dot(gall[block, :], w[:, lanes], preferred_element_type=F32)
        return out * gains[0:1, lanes] - xh[block, lanes].astype(F32) * gains[1:2, lanes] * coef

    sib_copies = []
    for j in range(CHUNKS):
        def to_sibling(i, j=j):
            i = i + j * (span // 512)
            bst[:, pl.ds(pl.multiple_of(i * 512, 512), 512)] = share((1 - c) * 128, i).astype(BF)

        tiles(span // 512, to_sibling)
        lanes = pl.ds(j * span, span)
        sib_copies.append(send(bst.at[:, lanes], brx.at[:, lanes], sibling))
    x_copies = []
    for j in range(CHUNKS):
        sib_copies[j].wait_recv()

        def to_x(i, j=j):
            i = i + j * (span // 512)
            lanes = pl.ds(pl.multiple_of(i * 512, 512), 512)
            out = share(c * 128, i) + brx[:, lanes].astype(F32)
            xown[:, lanes] = out
            xst[:, lanes] = out.astype(BF)

        tiles(span // 512, to_x)
        lanes = pl.ds(j * span, span)
        x_copies.append([
            send(xst.at[rows(xmod(k) * 32, 32), lanes], xrx.at[k - 1, :, lanes], x_peers[k - 1])
            for k in range(1, 4)
        ])
    mine32 = rows(x * 32, 32)
    z_copies = []
    for j in range(CHUNKS):
        lanes = pl.ds(j * span, span)
        for cp in x_copies[j]:
            cp.wait_recv()
        out = xown[mine32, lanes]
        for k in range(3):
            out = out + xrx[k, :, lanes].astype(F32)
        xown[mine32, lanes] = out
        zst[:, lanes] = out.astype(BF)
        z_copies.append([
            send(zst.at[:, piece(j, zmod(k))], zrx.at[k - 1, :, pl.ds(j * part, part)], z_peers[k - 1])
            for k in range(1, 8)
        ])
    ag = []
    for j in range(CHUNKS):
        lanes = piece(j, z)
        total = xown[mine32, lanes]
        for k in range(7):
            z_copies[j][k].wait_recv()
            total = total + zrx[k, :, pl.ds(j * part, part)].astype(F32)
        grad_out[place, lanes] = total.astype(BF)
        ag.append(gather_z(grad_out, j))
    xcop = []
    for j in range(CHUNKS):
        for cp in ag[j]:
            cp.wait_recv()
        xcop.append(gather_x(grad_out, j))
    for j in range(CHUNKS):
        forward(grad_out, j, *xcop[j])
    for j in range(CHUNKS):
        for cp in xcop[j][1]:
            cp.wait_recv()
    f_sib.wait_recv()
    f_fwd.wait_recv()
    for cp in started:
        cp.wait_send()


COPIES = 140


def on_device(
    frames, adapter_weight, text_embed, audio_len, text_len, norm_gain, gate_up, cotangent
):
    feat_here = frames.shape[2]
    width_here = adapter_weight.shape[2]
    units = 2 * gate_up.shape[2]
    depth = 4 * feat_here
    stacked = frames[0, : 4 * HEAD].reshape(HEAD, depth)
    kernel = adapter_weight.reshape(depth, width_here)
    gain = norm_gain.astype(F32)
    gains = jnp.stack([gain, 1.0 / gain])
    weights = jnp.transpose(gate_up, (1, 2, 0)).reshape(units, width_here)
    cot = cotangent.T
    vmem = pl.BlockSpec(memory_space=pltpu.VMEM)
    smem = pl.BlockSpec(memory_space=pltpu.SMEM)
    scratch = [
        ((PADDED, width_here), BF),
        ((256, width_here), BF),
        ((256, width_here), BF),
        ((HEAD, width_here), F32),
        ((32, width_here), BF),
        ((32, width_here), BF),
        ((32, width_here), BF),
        ((7, 32, width_here // 8), BF),
        ((256, PADDED), BF),
        ((256, PADDED), BF),
        ((6, HEAD, PADDED), BF),
        ((256, PADDED), BF),
        ((128, width_here), BF),
        ((128, width_here), BF),
        ((128, width_here), BF),
        ((128, width_here), F32),
        ((3, 32, width_here), BF),
        ((32, width_here), BF),
        ((7, 32, width_here // 8), BF),
    ]
    hidden, grad, all_frames = pl.pallas_call(
        fused_kernel,
        out_shape=(
            jax.ShapeDtypeStruct((units // 2, 128), BF),
            jax.ShapeDtypeStruct((256, width_here), BF),
            jax.ShapeDtypeStruct((256, depth), BF),
        ),
        in_specs=[smem, smem] + [vmem] * 5 + [pl.BlockSpec(memory_space=pl.ANY)],
        out_specs=(vmem, vmem, vmem),
        scratch_shapes=[pltpu.VMEM(s, t) for s, t in scratch]
        + [
            pltpu.SemaphoreType.DMA((COPIES,)),
            pltpu.SemaphoreType.DMA((COPIES,)),
            pltpu.SemaphoreType.DMA,
        ],
        compiler_params=pltpu.CompilerParams(
            collective_id=0, has_side_effects=True, vmem_limit_bytes=56 << 20
        ),
    )(audio_len, text_len, stacked, kernel, text_embed, gains, cot, weights)
    weight_grad = lax.dot_general(
        all_frames, grad, (((0,), (0,)), ((), ())), preferred_element_type=F32
    )
    return (hidden.T, weight_grad.reshape(4, feat_here, width_here))


def solution(mesh):
    return jax.shard_map(
        on_device,
        mesh=mesh,
        in_specs=(
            P("batch", None, "hidden"),
            P(None, "hidden", "width"),
            P("batch", "width"),
            P("batch"),
            P("batch"),
            P("width"),
            P("width", None, ("batch", "hidden")),
            P("width", ("batch", "hidden")),
        ),
        out_specs=(P("width", ("batch", "hidden")), P(None, "hidden", "width")),
        check_vma=False,
    )
```

```python
import jax
import jax.numpy as jnp
from jax import lax
from jax.experimental import pallas as pl
from jax.experimental.pallas import tpu as pltpu
from jax.sharding import PartitionSpec as P

D = 16384
HEAD = 64
PADDED = 896
CHUNKS = 4
COPIES = 96
norm_eps = 1e-05
MESH = pl.DeviceIdType.MESH
BF = jnp.bfloat16
F32 = jnp.float32
SUMS_A = BF
SUMS_B = F32


def fused_kernel(
    alen, tlen, frames, kernel, text, gain, cot, w_hbm,
    hidden_out, grad_out, frames_out,
    gains, w, xh, xt, taps, frm, pa, sta, rxa, stz, rza, stat_out, stat_in, gacc, tacc, sqs, gst, tst, grx,
    totals, gall, coefs, bst, brx, xst, xown, xrx, zst, zrx,
    send_sems, recv_sems, local_sem,
):
    batch, hid, y = (lax.axis_index(a) for a in ("batch", "hidden", "width"))
    xhi, c = batch // 2, batch % 2
    xlo, z = hid // 8, hid % 8
    x = xhi * 2 + xlo
    width = text.shape[1]
    feat = kernel.shape[1]
    units = w_hbm.shape[0]
    half = units // 2
    span = width // CHUNKS
    part = span // 8

    def device(x_=x, c_=c, z_=z, y_=y):
        return {"batch": (x_ // 2) * 2 + c_, "hidden": (x_ % 2) * 8 + z_, "width": y_}

    def zmod(k):
        return lax.rem(z + k, 8)

    def xmod(k):
        return lax.rem(x + k, 4)

    def ymod(k):
        return lax.rem(y + k, 4)

    def slot(seq):
        return (seq % 2) * 2 + seq // 2

    sibling = device(c_=1 - c)
    pair = device(x_=xhi * 2 + 1 - xlo)
    cross = device(x_=(1 - xhi) * 2 + 1 - xlo)
    far = device(x_=(1 - xhi) * 2 + xlo)
    z_peers = [device(z_=zmod(k)) for k in range(1, 8)]
    x_peers = [device(x_=xmod(k)) for k in range(1, 4)]
    y_peers = [device(y_=ymod(k)) for k in range(1, 4)]

    barrier = pltpu.get_barrier_semaphore()
    peers = [sibling] + z_peers + x_peers + y_peers
    for p in peers:
        pl.semaphore_signal(barrier, inc=1, device_id=p, device_id_type=MESH)

    groups = []
    landed = set()

    def group(ref, copies):
        i = len(groups)

        def describe(src, dst, peer):
            return pltpu.make_async_remote_copy(
                src_ref=src, dst_ref=dst, send_sem=send_sems.at[i], recv_sem=recv_sems.at[i],
                device_id=peer, device_id_type=MESH,
            )

        for src, dst, peer in copies:
            describe(src, dst, peer).start()
        groups.append(describe(ref, ref, copies[0][2]))
        return i

    def send(src, dst, peer):
        return group(dst, [(src, dst, peer)])

    def arrive(i):
        if i not in landed:
            landed.add(i)
            groups[i].wait_recv()

    def arrive_local():
        if "w" not in landed:
            landed.add("w")
            w_copy.wait()

    def finish():
        arrive_local()
        for i in range(len(groups)):
            arrive(i)
        for copy in groups:
            copy.wait_send()

    w_copy = pltpu.make_async_copy(w_hbm, w.at[pl.ds(0, units)], local_sem)
    w_copy.start()

    def rows(start, size):
        return pl.ds(pl.multiple_of(start, size), size)

    def columns(j):
        return pl.ds(j * span, span)

    def piece(j, who):
        return pl.ds(pl.multiple_of(j * span + who * part, part), part)

    def tiles(count, body):
        def step(i, carry):
            body(i)
            return carry

        lax.fori_loop(0, count, step, 0)

    def lanes_of(i, size):
        return pl.ds(pl.multiple_of(i * size, size), size)

    want = lax.broadcasted_iota(jnp.int32, (4 * HEAD, 4 * HEAD), 0)
    have = lax.broadcasted_iota(jnp.int32, (4 * HEAD, 4 * HEAD), 1)
    pick = jnp.where(have == 4 * (want % HEAD) + want // HEAD, 1.0, 0.0).astype(BF)
    taps[...] = lax.dot_general(
        pick, frames[:, 0 : 4 * HEAD], (((1,), (1,)), ((), ())), preferred_element_type=F32
    ).astype(BF)

    def audio_tile(i):
        lanes = lanes_of(i, 512)
        out = jnp.dot(taps[0:HEAD], kernel[0, :, lanes], preferred_element_type=F32)
        for tap in range(1, 4):
            out += jnp.dot(
                taps[tap * HEAD : (tap + 1) * HEAD], kernel[tap, :, lanes], preferred_element_type=F32
            )
        pa[:, lanes] = out

    own_rows = rows(32 * xlo, 32)
    other_rows = rows(32 * (1 - xlo), 32)
    pair_copies = []
    for j in range(CHUNKS):
        for i in range(span // 512):
            audio_tile(j * (span // 512) + i)
        sta[:, columns(j)] = pa[other_rows, columns(j)].astype(BF)
        if j == 0:
            pl.semaphore_wait(barrier, len(peers))
        pair_copies.append(send(sta.at[:, columns(j)], rxa.at[:, columns(j)], pair))

    audio_count = alen[0]
    filled = alen[0] + tlen[0]
    me = slot(batch)
    mine = rows(me * HEAD, HEAD)
    theirs = rows(slot((1 - xhi) * 2 + c) * HEAD, HEAD)

    def square(i, acc):
        v = text[:, lanes_of(i, 128)].astype(F32)
        return acc + v * v

    squares = lax.fori_loop(0, width // 128, square, jnp.zeros((128, 128), F32))
    squares = jnp.broadcast_to(jnp.sum(squares, axis=1, keepdims=True), (128, 128))
    stat_out[...] = squares.T[:8]
    stat_copies = group(stat_in, [(stat_out, stat_in.at[k - 1], y_peers[k - 1]) for k in range(1, 4)])
    head_pos = lax.broadcasted_iota(jnp.int32, (HEAD, 1), 0)
    lane64 = lax.broadcasted_iota(jnp.int32, (HEAD, 128), 1)
    is_audio = head_pos < audio_count
    frm[mine, :] = jnp.where(
        jnp.logical_and(is_audio, lax.broadcasted_iota(jnp.int32, (HEAD, 512), 1) == 127), 1.0, 0.0
    ).astype(BF)
    for tap in range(4):
        block = taps[tap * HEAD : (tap + 1) * HEAD]
        frm[mine, tap * 128 : tap * 128 + feat] = jnp.where(is_audio, block, jnp.zeros_like(block))
    f_far = send(frm.at[mine], frm.at[mine], far)
    f_sib = send(frm.at[mine], frm.at[mine], sibling)
    gain_vals = gain[...].astype(F32)
    for i in range(width // 128):
        gains[0:1, i * 128 : (i + 1) * 128] = gain_vals[i : i + 1]
    gains[1:2, :] = 1.0 / gains[0:1, :]
    arrive(stat_copies)
    stat = stat_out[...] + stat_in[0] + stat_in[1] + stat_in[2]
    inv_text = lax.rsqrt(stat[0:1] / D + norm_eps)
    inv_text = jnp.broadcast_to(inv_text, (128, 128)).T
    totals[:, 0:128] = inv_text

    place = rows(c * 128 + x * 32, 32)
    pos = lax.broadcasted_iota(jnp.int32, (32, 1), 0) + 32 * xlo

    def gather_z(buf, j):
        own = buf.at[place, piece(j, z)]
        return group(buf.at[place, pl.ds(j * span, 7 * part)], [(own, own, p) for p in z_peers])

    def gather_x(buf, j):
        own = buf.at[place, columns(j)]
        right = send(own, own, x_peers[0])
        left = send(own, own, x_peers[2])
        direct = send(own, own, x_peers[1]) if j == CHUNKS - 1 else None
        return right, left, direct

    def hand_on(buf, j, right, left, direct):
        before = c * 128 + xmod(3) * 32
        after = c * 128 + xmod(1) * 32
        arrive(right)
        arrive(left)
        if direct is None:
            low = buf.at[rows(before, 16), columns(j)]
            high = buf.at[rows(after + 16, 16), columns(j)]
            both = buf.at[rows(c * 128 + xmod(2) * 32, 32), columns(j)]
            direct = group(both, [(low, low, x_peers[0]), (high, high, x_peers[2])])
        return direct

    def to_core(buf, j, direct):
        arrive(direct)
        half_rows = buf.at[rows(c * 128, 128), columns(j)]
        return send(half_rows, half_rows, sibling)

    def scatter_z(stage, landing, j):
        lanes = pl.ds(j * part, part)
        return group(
            landing.at[:, :, lanes],
            [(stage.at[:, piece(j, zmod(k))], landing.at[k - 1, :, lanes], z_peers[k - 1]) for k in range(1, 8)],
        )

    def pipeline(buf, order, first, second, last, extra):
        live = {}
        for t in range(CHUNKS + max(lag for _, lag in order)):
            for stage, lag in order:
                j = t - lag
                if j < 0 or j >= CHUNKS:
                    continue
                if stage == 0:
                    live[j] = first(j)
                elif stage == 1:
                    second(j, live[j])
                    live[j] = gather_z(buf, j)
                elif stage == 2:
                    arrive(live[j])
                    live[j] = gather_x(buf, j)
                elif stage == 3:
                    live[j] = hand_on(buf, j, *live[j])
                elif stage == 4:
                    live[j] = to_core(buf, j, live[j])
                else:
                    arrive(live[j])
                    last(j)
            extra(t)

    def pair_sum(j):
        arrive(pair_copies[j])
        out = pa[own_rows, columns(j)] + rxa[:, columns(j)].astype(F32)
        pa[own_rows, columns(j)] = out
        stz[:, columns(j)] = out.astype(stz.dtype)
        return scatter_z(stz, rza, j)

    def head_stream(j, copies):
        arrive(copies)
        lanes = piece(j, z)
        total = pa[own_rows, lanes]
        for k in range(7):
            total = total + rza[k, :, pl.ds(j * part, part)].astype(F32)
        words = text[own_rows, lanes].astype(F32) * totals[own_rows, 0:1]
        stream = jnp.where(pos < audio_count, total, jnp.where(pos < filled, words, 0.0))
        xh[place, lanes] = (stream * gains[0:1, lanes]).astype(BF)

    def project(buf, acc, j):
        lanes = columns(j)
        for start in range(0, PADDED, 256):
            size = min(256, PADDED - start)
            out = lax.dot_general(
                buf[:, lanes], w[pl.ds(start, size), lanes], (((1,), (1,)), ((), ())),
                preferred_element_type=F32,
            )
            if j == 0:
                acc[:, pl.ds(start, size)] = out
            else:
                acc[:, pl.ds(start, size)] += out

    def head_project(j):
        if j == 0:
            arrive_local()
            w[pl.ds(units, PADDED - units), :] = jnp.zeros((PADDED - units, width), BF)
            sqs[...] = jnp.zeros_like(sqs)

        def head_square(i, carry):
            lanes = lanes_of(j * (span // 128) + i, 128)
            v = xh[:, lanes].astype(F32) * gains[1:2, lanes]
            sqs[...] += v * v
            return carry

        lax.fori_loop(0, span // 128, head_square, 0)
        project(xh, gacc, j)

    def tail_tile(i):
        lanes = lanes_of(i, 512)
        vals = text[HEAD:, lanes].astype(F32) * totals[HEAD:, 0:1]
        xt[mine, lanes] = (jnp.where((head_pos + HEAD) < filled, vals, 0.0) * gains[0:1, lanes]).astype(BF)

    def during_head(t):
        if t == CHUNKS:
            tiles(width // 512, tail_tile)

    pipeline(xh, ((1, 2), (0, 0), (2, 3), (3, 4), (4, 5), (5, 6)), pair_sum, head_stream, head_project, during_head)
    lane256 = lax.broadcasted_iota(jnp.int32, (256, 128), 1)
    mark = units - (PADDED - 128)
    last_tile = pl.ds(PADDED - 128, 128)
    sq = jnp.sum(sqs[...], axis=1, keepdims=True)
    high = sq.astype(BF).astype(F32)
    gacc[:, last_tile] = jnp.where(
        lane256 == mark, high, jnp.where(lane256 == mark + 1, sq - high, gacc[:, last_tile])
    )

    def spread(acc, stage, base):
        stage[...] = acc[...].astype(BF)
        return group(
            grx.at[base : base + 3],
            [
                (stage.at[rows(slot(ymod(k)) * HEAD, HEAD)], grx.at[base + k - 1], y_peers[k - 1])
                for k in (2, 1, 3)
            ],
        )

    head_y = spread(gacc, gst, 0)
    cross_copy = send(xt.at[mine], xt.at[mine], cross)
    tail_sib = send(xt.at[mine], xt.at[mine], sibling)
    arrive(f_far)
    f_fwd = send(frm.at[theirs], frm.at[theirs], sibling)
    arrive(f_sib)
    arrive(f_fwd)
    arrive(head_y)

    keep = rows(slot(y) * HEAD, HEAD)

    def total_of(acc, base):
        t = acc[keep, :]
        for k in range(3):
            t = t + grx[base + k].astype(F32)
        return t

    totals[0:HEAD, :] = total_of(gacc, 0)
    totals[HEAD:, :] = jnp.zeros((128 - HEAD, PADDED), F32)
    flag = frm[keep, 0:128].astype(F32)[:, 127:128]
    totals[0:HEAD, last_tile] = jnp.where(lane64 == mark + 2, flag, totals[0:HEAD, last_tile])

    def activations():
        both = totals[...].T
        stat = both[units : units + 8]
        inv = jnp.where(stat[2:3] > 0.5, lax.rsqrt((stat[0:1] + stat[1:2]) / D + norm_eps), 1.0)
        gate = both[:half] * inv
        up = both[half:units] * inv
        sig = jax.nn.sigmoid(gate)
        return inv, gate, up, sig, gate * sig

    inv, gate, up, sig, silu = activations()
    cotv = cot[...].astype(F32)
    g_gate = cotv * up * sig * (1.0 + gate * (1.0 - sig))
    g_up = cotv * silu
    inner = jnp.sum(g_gate * gate + g_up * up, axis=0, keepdims=True) * (inv * inv) / D
    high = inner.astype(BF).astype(F32)
    row = lax.broadcasted_iota(jnp.int32, (PADDED - units, 128), 0)
    extra_rows = jnp.where(row == 0, high, jnp.where(row == 1, inner - high, 0.0))
    grads = jnp.concatenate([g_gate * inv, g_up * inv, extra_rows], axis=0).T
    gall[keep, :] = grads[:HEAD].astype(BF)
    g_copies = group(gall.at[0 : 3 * HEAD], [(gall.at[keep], gall.at[keep], p) for p in y_peers])
    frames_t = frm[...].T
    for tap in range(4):
        frames_out[tap * feat : (tap + 1) * feat] = frames_t[tap * 128 : tap * 128 + feat]
    arrive(g_copies)

    edge = gall[:, last_tile].astype(F32)
    marked = jnp.logical_or(lane256 == mark, lane256 == mark + 1)
    coefs[...] = jnp.broadcast_to(
        jnp.sum(jnp.where(marked, edge, 0.0), axis=1, keepdims=True), (256, 128)
    )

    def share(base, lanes):
        block = rows(base, 128)
        out = jnp.dot(gall[block, :], w[:, lanes], preferred_element_type=F32)
        unit = xh[block, lanes].astype(F32) * gains[1:2, lanes]
        return out * gains[0:1, lanes] - unit * coefs[block, 0:1]

    sib_copies, x_copies = {}, {}

    def to_sibling(j):
        def tile(i):
            lanes = lanes_of(j * (span // 512) + i, 512)
            bst[:, lanes] = share((1 - c) * 128, lanes).astype(BF)

        tiles(span // 512, tile)
        sib_copies[j] = send(bst.at[:, columns(j)], brx.at[:, columns(j)], sibling)

    def to_x(j):
        arrive(sib_copies[j])

        def tile(i):
            lanes = lanes_of(j * (span // 512) + i, 512)
            out = share(c * 128, lanes) + brx[:, lanes].astype(F32)
            xown[:, lanes] = out
            xst[:, lanes] = out.astype(BF)

        tiles(span // 512, tile)
        x_copies[j] = group(
            xrx.at[:, :, columns(j)],
            [
                (xst.at[rows(xmod(k) * 32, 32), columns(j)], xrx.at[k - 1, :, columns(j)], x_peers[k - 1])
                for k in (2, 1, 3)
            ],
        )

    to_sibling(0)
    for j in range(CHUNKS):
        if j + 1 < CHUNKS:
            to_sibling(j + 1)
        to_x(j)
    arrive(cross_copy)
    tail_fwd = send(xt.at[theirs], xt.at[theirs], sibling)
    mine32 = rows(x * 32, 32)

    def x_sum(j):
        arrive(x_copies[j])
        out = xown[mine32, columns(j)]
        for k in range(3):
            out = out + xrx[k, :, columns(j)].astype(F32)
        xown[mine32, columns(j)] = out
        zst[:, columns(j)] = out.astype(zst.dtype)
        return scatter_z(zst, zrx, j)

    def head_grad(j, copies):
        arrive(copies)
        lanes = piece(j, z)
        total = xown[mine32, lanes]
        for k in range(7):
            total = total + zrx[k, :, pl.ds(j * part, part)].astype(F32)
        grad_out[place, lanes] = total.astype(BF)

    tail_y = []

    def during_tail(t):
        if t < CHUNKS:
            if t == 0:
                arrive(tail_sib)
                arrive(tail_fwd)
            project(xt, tacc, t)
        if t == CHUNKS - 1:
            tail_y.append(spread(tacc, tst, 3))
        if t == CHUNKS + 2:
            arrive(tail_y[0])
            totals[HEAD:, :] = total_of(tacc, 3)
            _, _, up, _, silu = activations()
            hidden_out[...] = (silu * up).astype(BF)

    pipeline(grad_out, ((0, 0), (1, 1), (2, 2), (3, 3), (4, 4), (5, 5)), x_sum, head_grad, lambda j: None, during_tail)
    finish()


def weight_kernel(frames_t, grad, out):
    feat = out.shape[1]
    total = jnp.dot(frames_t[...], grad[...], preferred_element_type=F32)
    for tap in range(4):
        out[tap] = total[tap * feat : (tap + 1) * feat]


def on_device(
    frames, adapter_weight, text_embed, audio_len, text_len, norm_gain, gate_up, cotangent
):
    feat_here = frames.shape[2]
    width_here = adapter_weight.shape[2]
    units = 2 * gate_up.shape[2]
    depth = 4 * feat_here
    gain = norm_gain.reshape(width_here // 128, 128)
    weights = jnp.transpose(gate_up, (1, 2, 0)).reshape(units, width_here)
    cot = cotangent.T
    vmem = pl.BlockSpec(memory_space=pltpu.VMEM)
    smem = pl.BlockSpec(memory_space=pltpu.SMEM)
    scratch = [
        ((2, width_here), F32),
        ((PADDED, width_here), BF),
        ((256, width_here), BF),
        ((256, width_here), BF),
        ((4 * HEAD, feat_here), BF),
        ((256, 512), BF),
        ((HEAD, width_here), F32),
        ((32, width_here), BF),
        ((32, width_here), BF),
        ((32, width_here), SUMS_A),
        ((7, 32, width_here // 8), SUMS_A),
        ((8, 128), F32),
        ((3, 8, 128), F32),
        ((256, PADDED), F32),
        ((256, PADDED), F32),
        ((256, 128), F32),
        ((256, PADDED), BF),
        ((256, PADDED), BF),
        ((6, HEAD, PADDED), BF),
        ((128, PADDED), F32),
        ((256, PADDED), BF),
        ((256, 128), F32),
        ((128, width_here), BF),
        ((128, width_here), BF),
        ((128, width_here), BF),
        ((128, width_here), F32),
        ((3, 32, width_here), BF),
        ((32, width_here), SUMS_B),
        ((7, 32, width_here // 8), SUMS_B),
    ]
    hidden, grad, frames_t = pl.pallas_call(
        fused_kernel,
        out_shape=(
            jax.ShapeDtypeStruct((units // 2, 128), BF),
            jax.ShapeDtypeStruct((256, width_here), BF),
            jax.ShapeDtypeStruct((depth, 256), BF),
        ),
        in_specs=[smem, smem] + [vmem] * 5 + [pl.BlockSpec(memory_space=pl.ANY)],
        out_specs=(vmem, vmem, vmem),
        scratch_shapes=[pltpu.VMEM(s, t) for s, t in scratch]
        + [
            pltpu.SemaphoreType.DMA((COPIES,)),
            pltpu.SemaphoreType.DMA((COPIES,)),
            pltpu.SemaphoreType.DMA,
        ],
        compiler_params=pltpu.CompilerParams(
            collective_id=0, has_side_effects=True, vmem_limit_bytes=56 << 20
        ),
    )(audio_len, text_len, frames[0].T, adapter_weight, text_embed, gain, cot, weights)
    tile = width_here // 4
    weight_grad = pl.pallas_call(
        weight_kernel,
        grid=(width_here // tile,),
        out_shape=jax.ShapeDtypeStruct((4, feat_here, width_here), F32),
        in_specs=[
            pl.BlockSpec((depth, 256), lambda i: (0, 0)),
            pl.BlockSpec((256, tile), lambda i: (0, i)),
        ],
        out_specs=pl.BlockSpec((4, feat_here, tile), lambda i: (0, 0, i)),
    )(frames_t, grad)
    return (hidden.T, weight_grad)


def solution(mesh):
    return jax.shard_map(
        on_device,
        mesh=mesh,
        in_specs=(
            P("batch", None, "hidden"),
            P(None, "hidden", "width"),
            P("batch", "width"),
            P("batch"),
            P("batch"),
            P("width"),
            P("width", None, ("batch", "hidden")),
            P("width", ("batch", "hidden")),
        ),
        out_specs=(P("width", ("batch", "hidden")), P(None, "hidden", "width")),
        check_vma=False,
    )
```

```python
import jax
import jax.numpy as jnp
from jax import lax
from jax.experimental import pallas as pl
from jax.experimental.pallas import tpu as pltpu
from jax.sharding import PartitionSpec as P

D = 16384
HEAD = 64
PADDED = 896
CHUNKS = 4
COPIES = 84
Z_FIRST = 2
MADE = (0, 2, 1, 3)
norm_eps = 1e-05
MESH = pl.DeviceIdType.MESH
BF = jnp.bfloat16
F32 = jnp.float32
SUMS_A = BF
SUMS_B = F32


def fused_kernel(
    alen, tlen, frames, kernel, text, gain, cot, w_hbm,
    hidden_out, grad_out, frames_out,
    gains, w, xh, xt, taps, frm, pa, sta, rxa, stz, rza, stat_out, stat_in, gacc, tacc, sqs, gst, tst, grx,
    totals, gall, coefs, bst, brx, xst, xown, xrx, zst, zrx, zfirst,
    send_sems, recv_sems, local_sem,
):
    batch, hid, y = (lax.axis_index(a) for a in ("batch", "hidden", "width"))
    xhi, c = batch // 2, batch % 2
    xlo, z = hid // 8, hid % 8
    x = xhi * 2 + xlo
    width = text.shape[1]
    feat = kernel.shape[1]
    units = w_hbm.shape[0]
    half = units // 2
    span = width // CHUNKS
    part = span // 8

    def device(x_=x, c_=c, z_=z, y_=y):
        return {"batch": (x_ // 2) * 2 + c_, "hidden": (x_ % 2) * 8 + z_, "width": y_}

    def zmod(k):
        return lax.rem(z + k, 8)

    def xmod(k):
        return lax.rem(x + k, 4)

    def ymod(k):
        return lax.rem(y + k, 4)

    def slot(seq):
        return (seq % 2) * 2 + seq // 2

    sibling = device(c_=1 - c)
    pair = device(x_=xhi * 2 + 1 - xlo)
    cross = device(x_=(1 - xhi) * 2 + 1 - xlo)
    far = device(x_=(1 - xhi) * 2 + xlo)
    z_peers = [device(z_=zmod(k)) for k in range(1, 8)]
    x_peers = [device(x_=xmod(k)) for k in range(1, 4)]
    y_peers = [device(y_=ymod(k)) for k in range(1, 4)]

    barrier = pltpu.get_barrier_semaphore()
    peers = [sibling] + z_peers + x_peers + y_peers
    for p in peers:
        pl.semaphore_signal(barrier, inc=1, device_id=p, device_id_type=MESH)

    groups = []
    landed = set()

    def group(ref, copies):
        i = len(groups)

        def describe(src, dst, peer):
            return pltpu.make_async_remote_copy(
                src_ref=src, dst_ref=dst, send_sem=send_sems.at[i], recv_sem=recv_sems.at[i],
                device_id=peer, device_id_type=MESH,
            )

        for src, dst, peer in copies:
            describe(src, dst, peer).start()
        groups.append(describe(ref, ref, copies[0][2]))
        return i

    def send(src, dst, peer):
        return group(dst, [(src, dst, peer)])

    def arrive(i):
        if i not in landed:
            landed.add(i)
            groups[i].wait_recv()

    def arrive_local():
        if "w" not in landed:
            landed.add("w")
            w_copy.wait()

    def finish():
        arrive_local()
        for i in range(len(groups)):
            arrive(i)
        for copy in groups:
            copy.wait_send()

    w_copy = pltpu.make_async_copy(w_hbm, w.at[pl.ds(0, units)], local_sem)
    w_copy.start()

    def rows(start, size):
        return pl.ds(pl.multiple_of(start, size), size)

    def columns(j):
        return pl.ds(j * span, span)

    def piece(j, who):
        return pl.ds(pl.multiple_of(j * span + who * part, part), part)

    def tiles(count, body):
        def step(i, carry):
            body(i)
            return carry

        lax.fori_loop(0, count, step, 0)

    def lanes_of(i, size):
        return pl.ds(pl.multiple_of(i * size, size), size)

    want = lax.broadcasted_iota(jnp.int32, (4 * HEAD, 4 * HEAD), 0)
    have = lax.broadcasted_iota(jnp.int32, (4 * HEAD, 4 * HEAD), 1)
    pick = jnp.where(have == 4 * (want % HEAD) + want // HEAD, 1.0, 0.0).astype(BF)
    taps[...] = lax.dot_general(
        pick, frames[:, 0 : 4 * HEAD], (((1,), (1,)), ((), ())), preferred_element_type=F32
    ).astype(BF)

    def audio_tile(i):
        lanes = lanes_of(i, 512)
        out = jnp.dot(taps[0:HEAD], kernel[0, :, lanes], preferred_element_type=F32)
        for tap in range(1, 4):
            out += jnp.dot(
                taps[tap * HEAD : (tap + 1) * HEAD], kernel[tap, :, lanes], preferred_element_type=F32
            )
        pa[:, lanes] = out

    own_rows = rows(32 * xlo, 32)
    other_rows = rows(32 * (1 - xlo), 32)
    pair_copies = []
    for j in range(CHUNKS):
        for i in range(span // 512):
            audio_tile(j * (span // 512) + i)
        sta[:, columns(j)] = pa[other_rows, columns(j)].astype(BF)
        if j == 0:
            pl.semaphore_wait(barrier, len(peers))
        pair_copies.append(send(sta.at[:, columns(j)], rxa.at[:, columns(j)], pair))

    audio_count = alen[0]
    filled = alen[0] + tlen[0]
    me = slot(batch)
    mine = rows(me * HEAD, HEAD)
    theirs = rows(slot((1 - xhi) * 2 + c) * HEAD, HEAD)

    def square(i, acc):
        v = text[:, lanes_of(i, 128)].astype(F32)
        return acc + v * v

    squares = lax.fori_loop(0, width // 128, square, jnp.zeros((128, 128), F32))
    squares = jnp.broadcast_to(jnp.sum(squares, axis=1, keepdims=True), (128, 128))
    stat_out[...] = squares.T[:8]
    stat_copies = group(stat_in, [(stat_out, stat_in.at[k - 1], y_peers[k - 1]) for k in range(1, 4)])
    head_pos = lax.broadcasted_iota(jnp.int32, (HEAD, 1), 0)
    lane64 = lax.broadcasted_iota(jnp.int32, (HEAD, 128), 1)
    is_audio = head_pos < audio_count
    frm[mine, :] = jnp.where(
        jnp.logical_and(is_audio, lax.broadcasted_iota(jnp.int32, (HEAD, 512), 1) == 127), 1.0, 0.0
    ).astype(BF)
    for tap in range(4):
        block = taps[tap * HEAD : (tap + 1) * HEAD]
        frm[mine, tap * 128 : tap * 128 + feat] = jnp.where(is_audio, block, jnp.zeros_like(block))
    f_far = send(frm.at[mine], frm.at[mine], far)
    f_sib = send(frm.at[mine], frm.at[mine], sibling)
    gain_vals = gain[...].astype(F32)
    for i in range(width // 128):
        gains[0:1, i * 128 : (i + 1) * 128] = gain_vals[i : i + 1]
    gains[1:2, :] = 1.0 / gains[0:1, :]
    arrive(stat_copies)
    stat = stat_out[...] + stat_in[0] + stat_in[1] + stat_in[2]
    inv_text = lax.rsqrt(stat[0:1] / D + norm_eps)
    inv_text = jnp.broadcast_to(inv_text, (128, 128)).T
    totals[:, 0:128] = inv_text

    place = rows(c * 128 + x * 32, 32)
    pos = lax.broadcasted_iota(jnp.int32, (32, 1), 0) + 32 * xlo

    def gather_z(buf, j):
        own = buf.at[place, piece(j, z)]
        return group(buf.at[place, pl.ds(j * span, 7 * part)], [(own, own, p) for p in z_peers])

    def gather_x(buf, j):
        own = buf.at[place, columns(j)]
        right = send(own, own, x_peers[0])
        left = send(own, own, x_peers[2])
        direct = send(own, own, x_peers[1]) if j == CHUNKS - 1 else None
        return right, left, direct

    def hand_on(buf, j, right, left, direct):
        before = c * 128 + xmod(3) * 32
        after = c * 128 + xmod(1) * 32
        arrive(right)
        arrive(left)
        if direct is None:
            low = buf.at[rows(before, 16), columns(j)]
            high = buf.at[rows(after + 16, 16), columns(j)]
            both = buf.at[rows(c * 128 + xmod(2) * 32, 32), columns(j)]
            direct = group(both, [(low, low, x_peers[0]), (high, high, x_peers[2])])
        return direct

    def to_core(buf, j, direct):
        arrive(direct)
        half_rows = buf.at[rows(c * 128, 128), columns(j)]
        return send(half_rows, half_rows, sibling)

    def scatter_z(stage, landing, j):
        lanes = pl.ds(j * part, part)
        return group(
            landing.at[:, :, lanes],
            [(stage.at[:, piece(j, zmod(k))], landing.at[k - 1, :, lanes], z_peers[k - 1]) for k in range(1, 8)],
        )

    def pipeline(buf, order, first, second, last, extra):
        live = {}
        for t in range(CHUNKS + max(lag for _, lag in order)):
            for stage, lag in order:
                j = t - lag
                if j < 0 or j >= CHUNKS:
                    continue
                if stage == 0:
                    live[j] = first(j)
                elif stage == 1:
                    second(j, live[j])
                    live[j] = gather_z(buf, j)
                elif stage == 2:
                    arrive(live[j])
                    live[j] = gather_x(buf, j)
                elif stage == 3:
                    live[j] = hand_on(buf, j, *live[j])
                elif stage == 4:
                    live[j] = to_core(buf, j, live[j])
                else:
                    arrive(live[j])
                    last(j)
            extra(t)

    def pair_sum(j):
        arrive(pair_copies[j])
        out = pa[own_rows, columns(j)] + rxa[:, columns(j)].astype(F32)
        pa[own_rows, columns(j)] = out
        stz[:, columns(j)] = out.astype(stz.dtype)
        return scatter_z(stz, rza, j)

    def head_stream(j, copies):
        arrive(copies)
        lanes = piece(j, z)
        total = pa[own_rows, lanes]
        for k in range(7):
            total = total + rza[k, :, pl.ds(j * part, part)].astype(F32)
        words = text[own_rows, lanes].astype(F32) * totals[own_rows, 0:1]
        stream = jnp.where(pos < audio_count, total, jnp.where(pos < filled, words, 0.0))
        xh[place, lanes] = (stream * gains[0:1, lanes]).astype(BF)

    def project(buf, acc, j):
        lanes = columns(j)
        for start in range(0, PADDED, 256):
            size = min(256, PADDED - start)
            out = lax.dot_general(
                buf[:, lanes], w[pl.ds(start, size), lanes], (((1,), (1,)), ((), ())),
                preferred_element_type=F32,
            )
            if j == 0:
                acc[:, pl.ds(start, size)] = out
            else:
                acc[:, pl.ds(start, size)] += out

    def head_project(j):
        if j == 0:
            arrive_local()
            w[pl.ds(units, PADDED - units), :] = jnp.zeros((PADDED - units, width), BF)
            sqs[...] = jnp.zeros_like(sqs)

        def head_square(i, carry):
            lanes = lanes_of(j * (span // 128) + i, 128)
            v = xh[:, lanes].astype(F32) * gains[1:2, lanes]
            sqs[...] += v * v
            return carry

        lax.fori_loop(0, span // 128, head_square, 0)
        project(xh, gacc, j)

    def tail_tile(i):
        lanes = lanes_of(i, 512)
        vals = text[HEAD:, lanes].astype(F32) * totals[HEAD:, 0:1]
        xt[mine, lanes] = (jnp.where((head_pos + HEAD) < filled, vals, 0.0) * gains[0:1, lanes]).astype(BF)

    def during_head(t):
        if t == CHUNKS:
            tiles(width // 512, tail_tile)

    pipeline(xh, ((1, 2), (0, 0), (2, 3), (3, 4), (4, 5), (5, 6)), pair_sum, head_stream, head_project, during_head)
    lane256 = lax.broadcasted_iota(jnp.int32, (256, 128), 1)
    mark = units - (PADDED - 128)
    last_tile = pl.ds(PADDED - 128, 128)
    sq = jnp.sum(sqs[...], axis=1, keepdims=True)
    high = sq.astype(BF).astype(F32)
    gacc[:, last_tile] = jnp.where(
        lane256 == mark, high, jnp.where(lane256 == mark + 1, sq - high, gacc[:, last_tile])
    )

    def spread(acc, stage, base):
        stage[...] = acc[...].astype(BF)
        return group(
            grx.at[base : base + 3],
            [
                (stage.at[rows(slot(ymod(k)) * HEAD, HEAD)], grx.at[base + k - 1], y_peers[k - 1])
                for k in (2, 1, 3)
            ],
        )

    head_y = spread(gacc, gst, 0)
    cross_copy = send(xt.at[mine], xt.at[mine], cross)
    tail_sib = send(xt.at[mine], xt.at[mine], sibling)
    arrive(f_far)
    f_fwd = send(frm.at[theirs], frm.at[theirs], sibling)
    arrive(f_sib)
    arrive(f_fwd)
    arrive(head_y)

    keep = rows(slot(y) * HEAD, HEAD)

    def total_of(acc, base):
        t = acc[keep, :]
        for k in range(3):
            t = t + grx[base + k].astype(F32)
        return t

    totals[0:HEAD, :] = total_of(gacc, 0)
    totals[HEAD:, :] = jnp.zeros((128 - HEAD, PADDED), F32)
    flag = frm[keep, 0:128].astype(F32)[:, 127:128]
    totals[0:HEAD, last_tile] = jnp.where(lane64 == mark + 2, flag, totals[0:HEAD, last_tile])

    def activations():
        both = totals[...].T
        stat = both[units : units + 8]
        inv = jnp.where(stat[2:3] > 0.5, lax.rsqrt((stat[0:1] + stat[1:2]) / D + norm_eps), 1.0)
        gate = both[:half] * inv
        up = both[half:units] * inv
        sig = jax.nn.sigmoid(gate)
        return inv, gate, up, sig, gate * sig

    inv, gate, up, sig, silu = activations()
    cotv = cot[...].astype(F32)
    g_gate = cotv * up * sig * (1.0 + gate * (1.0 - sig))
    g_up = cotv * silu
    inner = jnp.sum(g_gate * gate + g_up * up, axis=0, keepdims=True) * (inv * inv) / D
    high = inner.astype(BF).astype(F32)
    row = lax.broadcasted_iota(jnp.int32, (PADDED - units, 128), 0)
    extra_rows = jnp.where(row == 0, high, jnp.where(row == 1, inner - high, 0.0))
    grads = jnp.concatenate([g_gate * inv, g_up * inv, extra_rows], axis=0).T
    gall[keep, :] = grads[:HEAD].astype(BF)
    g_copies = group(gall.at[0 : 3 * HEAD], [(gall.at[keep], gall.at[keep], p) for p in y_peers])
    frames_t = frm[...].T
    for tap in range(4):
        frames_out[tap * feat : (tap + 1) * feat] = frames_t[tap * 128 : tap * 128 + feat]
    arrive(g_copies)

    edge = gall[:, last_tile].astype(F32)
    marked = jnp.logical_or(lane256 == mark, lane256 == mark + 1)
    coefs[...] = jnp.broadcast_to(
        jnp.sum(jnp.where(marked, edge, 0.0), axis=1, keepdims=True), (256, 128)
    )

    def share(base, lanes):
        block = rows(base, 128)
        out = jnp.dot(gall[block, :], w[:, lanes], preferred_element_type=F32)
        unit = xh[block, lanes].astype(F32) * gains[1:2, lanes]
        return out * gains[0:1, lanes] - unit * coefs[block, 0:1]

    sib_copies, x_copies = {}, {}

    def to_sibling(j):
        def tile(i):
            lanes = lanes_of(j * (span // 512) + i, 512)
            bst[:, lanes] = share((1 - c) * 128, lanes).astype(BF)

        tiles(span // 512, tile)
        sib_copies[j] = send(bst.at[:, columns(j)], brx.at[:, columns(j)], sibling)

    def to_x(j):
        arrive(sib_copies[j])

        def tile(i):
            lanes = lanes_of(j * (span // 512) + i, 512)
            out = share(c * 128, lanes) + brx[:, lanes].astype(F32)
            xown[:, lanes] = out
            xst[:, lanes] = out.astype(BF)

        tiles(span // 512, tile)
        if j == Z_FIRST:
            x_copies[j] = group(
                zfirst,
                [(xst.at[:, piece(j, zmod(k))], zfirst.at[k - 1], z_peers[k - 1]) for k in (4, 3, 5, 2, 6, 1, 7)],
            )
            return
        x_copies[j] = group(
            xrx.at[:, :, columns(j)],
            [
                (xst.at[rows(xmod(k) * 32, 32), columns(j)], xrx.at[k - 1, :, columns(j)], x_peers[k - 1])
                for k in (2, 1, 3)
            ],
        )

    to_sibling(MADE[0])
    for i in range(CHUNKS):
        if i + 1 < CHUNKS:
            to_sibling(MADE[i + 1])
        to_x(MADE[i])
    arrive(cross_copy)
    tail_fwd = send(xt.at[theirs], xt.at[theirs], sibling)
    mine32 = rows(x * 32, 32)

    def x_sum(j):
        arrive(x_copies[j])
        if j == Z_FIRST:
            lanes = piece(j, z)
            out = xown[:, lanes]
            for k in range(7):
                out = out + zfirst[k].astype(F32)
            xown[:, lanes] = out
            xst[:, lanes] = out.astype(BF)
            first_part = pl.ds(j * span, part)
            return group(
                xrx.at[:, :, first_part],
                [
                    (xst.at[rows(xmod(k) * 32, 32), lanes], xrx.at[k - 1, :, first_part], x_peers[k - 1])
                    for k in (2, 1, 3)
                ],
            )
        out = xown[mine32, columns(j)]
        for k in range(3):
            out = out + xrx[k, :, columns(j)].astype(F32)
        xown[mine32, columns(j)] = out
        zst[:, columns(j)] = out.astype(zst.dtype)
        return scatter_z(zst, zrx, j)

    def head_grad(j, copies):
        arrive(copies)
        lanes = piece(j, z)
        total = xown[mine32, lanes]
        if j == Z_FIRST:
            for k in range(3):
                total = total + xrx[k, :, pl.ds(j * span, part)].astype(F32)
        else:
            for k in range(7):
                total = total + zrx[k, :, pl.ds(j * part, part)].astype(F32)
        grad_out[place, lanes] = total.astype(BF)

    tail_y = []

    def during_tail(t):
        if t < CHUNKS:
            if t == 0:
                arrive(tail_sib)
                arrive(tail_fwd)
            project(xt, tacc, t)
        if t == CHUNKS - 1:
            tail_y.append(spread(tacc, tst, 3))
        if t == CHUNKS + 2:
            arrive(tail_y[0])
            totals[HEAD:, :] = total_of(tacc, 3)
            _, _, up, _, silu = activations()
            hidden_out[...] = (silu * up).astype(BF)

    pipeline(grad_out, ((0, 0), (1, 1), (2, 2), (3, 3), (4, 4), (5, 5)), x_sum, head_grad, lambda j: None, during_tail)
    finish()


def weight_kernel(frames_t, grad, out):
    feat = out.shape[1]
    total = jnp.dot(frames_t[...], grad[...], preferred_element_type=F32)
    for tap in range(4):
        out[tap] = total[tap * feat : (tap + 1) * feat]


def on_device(
    frames, adapter_weight, text_embed, audio_len, text_len, norm_gain, gate_up, cotangent
):
    feat_here = frames.shape[2]
    width_here = adapter_weight.shape[2]
    units = 2 * gate_up.shape[2]
    depth = 4 * feat_here
    gain = norm_gain.reshape(width_here // 128, 128)
    weights = jnp.transpose(gate_up, (1, 2, 0)).reshape(units, width_here)
    cot = cotangent.T
    vmem = pl.BlockSpec(memory_space=pltpu.VMEM)
    smem = pl.BlockSpec(memory_space=pltpu.SMEM)
    scratch = [
        ((2, width_here), F32),
        ((PADDED, width_here), BF),
        ((256, width_here), BF),
        ((256, width_here), BF),
        ((4 * HEAD, feat_here), BF),
        ((256, 512), BF),
        ((HEAD, width_here), F32),
        ((32, width_here), BF),
        ((32, width_here), BF),
        ((32, width_here), SUMS_A),
        ((7, 32, width_here // 8), SUMS_A),
        ((8, 128), F32),
        ((3, 8, 128), F32),
        ((256, PADDED), F32),
        ((256, PADDED), F32),
        ((256, 128), F32),
        ((256, PADDED), BF),
        ((256, PADDED), BF),
        ((6, HEAD, PADDED), BF),
        ((128, PADDED), F32),
        ((256, PADDED), BF),
        ((256, 128), F32),
        ((128, width_here), BF),
        ((128, width_here), BF),
        ((128, width_here), BF),
        ((128, width_here), F32),
        ((3, 32, width_here), BF),
        ((32, width_here), SUMS_B),
        ((7, 32, width_here // 8), SUMS_B),
        ((7, 128, width_here // (8 * CHUNKS)), BF),
    ]
    hidden, grad, frames_t = pl.pallas_call(
        fused_kernel,
        out_shape=(
            jax.ShapeDtypeStruct((units // 2, 128), BF),
            jax.ShapeDtypeStruct((256, width_here), BF),
            jax.ShapeDtypeStruct((depth, 256), BF),
        ),
        in_specs=[smem, smem] + [vmem] * 5 + [pl.BlockSpec(memory_space=pl.ANY)],
        out_specs=(vmem, vmem, vmem),
        scratch_shapes=[pltpu.VMEM(s, t) for s, t in scratch]
        + [
            pltpu.SemaphoreType.DMA((COPIES,)),
            pltpu.SemaphoreType.DMA((COPIES,)),
            pltpu.SemaphoreType.DMA,
        ],
        compiler_params=pltpu.CompilerParams(
            collective_id=0, has_side_effects=True, vmem_limit_bytes=56 << 20
        ),
    )(audio_len, text_len, frames[0].T, adapter_weight, text_embed, gain, cot, weights)
    tile = width_here // 4
    weight_grad = pl.pallas_call(
        weight_kernel,
        grid=(width_here // tile,),
        out_shape=jax.ShapeDtypeStruct((4, feat_here, width_here), F32),
        in_specs=[
            pl.BlockSpec((depth, 256), lambda i: (0, 0)),
            pl.BlockSpec((256, tile), lambda i: (0, i)),
        ],
        out_specs=pl.BlockSpec((4, feat_here, tile), lambda i: (0, 0, i)),
    )(frames_t, grad)
    return (hidden.T, weight_grad)


def solution(mesh):
    return jax.shard_map(
        on_device,
        mesh=mesh,
        in_specs=(
            P("batch", None, "hidden"),
            P(None, "hidden", "width"),
            P("batch", "width"),
            P("batch"),
            P("batch"),
            P("width"),
            P("width", None, ("batch", "hidden")),
            P("width", ("batch", "hidden")),
        ),
        out_specs=(P("width", ("batch", "hidden")), P(None, "hidden", "width")),
        check_vma=False,
    )
```

```python
import jax
import jax.numpy as jnp
from jax import lax
from jax.experimental import pallas as pl
from jax.experimental.pallas import tpu as pltpu
from jax.sharding import PartitionSpec as P

D = 16384
HEAD = 64
PADDED = 896
CHUNKS = 4
COPIES = 84
norm_eps = 1e-05
MESH = pl.DeviceIdType.MESH
BF = jnp.bfloat16
F32 = jnp.float32
SUMS_A = BF
SUMS_B = BF


def fused_kernel(
    alen, tlen, frames, kernel, text, gain, cot, w_hbm,
    hidden_out, grad_out, frames_out,
    gains, w, xh, xt, taps, frm, pa, sta, rxa, stz, rza, stat_out, stat_in, gacc, tacc, sqs, gst, tst, grx,
    totals, gall, coefs, bst, brx, xst, xown, xrx, zst, zrx,
    send_sems, recv_sems, local_sem,
):
    batch, hid, y = (lax.axis_index(a) for a in ("batch", "hidden", "width"))
    xhi, c = batch // 2, batch % 2
    xlo, z = hid // 8, hid % 8
    x = xhi * 2 + xlo
    width = text.shape[1]
    feat = kernel.shape[1]
    units = w_hbm.shape[0]
    half = units // 2
    span = width // CHUNKS
    part = span // 8

    def device(x_=x, c_=c, z_=z, y_=y):
        return {"batch": (x_ // 2) * 2 + c_, "hidden": (x_ % 2) * 8 + z_, "width": y_}

    def zmod(k):
        return lax.rem(z + k, 8)

    def xmod(k):
        return lax.rem(x + k, 4)

    def ymod(k):
        return lax.rem(y + k, 4)

    def slot(seq):
        return (seq % 2) * 2 + seq // 2

    sibling = device(c_=1 - c)
    pair = device(x_=xhi * 2 + 1 - xlo)
    cross = device(x_=(1 - xhi) * 2 + 1 - xlo)
    far = device(x_=(1 - xhi) * 2 + xlo)
    z_peers = [device(z_=zmod(k)) for k in range(1, 8)]
    x_peers = [device(x_=xmod(k)) for k in range(1, 4)]
    y_peers = [device(y_=ymod(k)) for k in range(1, 4)]

    barrier = pltpu.get_barrier_semaphore()
    peers = [sibling] + z_peers + x_peers + y_peers
    for p in peers:
        pl.semaphore_signal(barrier, inc=1, device_id=p, device_id_type=MESH)

    groups = []
    landed = set()

    def group(ref, copies):
        i = len(groups)

        def describe(src, dst, peer):
            return pltpu.make_async_remote_copy(
                src_ref=src, dst_ref=dst, send_sem=send_sems.at[i], recv_sem=recv_sems.at[i],
                device_id=peer, device_id_type=MESH,
            )

        for src, dst, peer in copies:
            describe(src, dst, peer).start()
        groups.append(describe(ref, ref, copies[0][2]))
        return i

    def send(src, dst, peer):
        return group(dst, [(src, dst, peer)])

    def arrive(i):
        if i not in landed:
            landed.add(i)
            groups[i].wait_recv()

    def arrive_local():
        if "w" not in landed:
            landed.add("w")
            w_copy.wait()

    def finish():
        arrive_local()
        for i in range(len(groups)):
            arrive(i)
        for copy in groups:
            copy.wait_send()

    w_copy = pltpu.make_async_copy(w_hbm, w.at[pl.ds(0, units)], local_sem)
    w_copy.start()

    def rows(start, size):
        return pl.ds(pl.multiple_of(start, size), size)

    def columns(j):
        return pl.ds(j * span, span)

    def piece(j, who):
        return pl.ds(pl.multiple_of(j * span + who * part, part), part)

    def tiles(count, body):
        def step(i, carry):
            body(i)
            return carry

        lax.fori_loop(0, count, step, 0)

    def lanes_of(i, size):
        return pl.ds(pl.multiple_of(i * size, size), size)

    want = lax.broadcasted_iota(jnp.int32, (4 * HEAD, 4 * HEAD), 0)
    have = lax.broadcasted_iota(jnp.int32, (4 * HEAD, 4 * HEAD), 1)
    pick = jnp.where(have == 4 * (want % HEAD) + want // HEAD, 1.0, 0.0).astype(BF)
    taps[...] = lax.dot_general(
        pick, frames[:, 0 : 4 * HEAD], (((1,), (1,)), ((), ())), preferred_element_type=F32
    ).astype(BF)

    def audio_tile(i):
        lanes = lanes_of(i, 512)
        out = jnp.dot(taps[0:HEAD], kernel[0, :, lanes], preferred_element_type=F32)
        for tap in range(1, 4):
            out += jnp.dot(
                taps[tap * HEAD : (tap + 1) * HEAD], kernel[tap, :, lanes], preferred_element_type=F32
            )
        pa[:, lanes] = out

    own_rows = rows(32 * xlo, 32)
    other_rows = rows(32 * (1 - xlo), 32)
    pair_copies = []
    for j in range(CHUNKS):
        for i in range(span // 512):
            audio_tile(j * (span // 512) + i)
        sta[:, columns(j)] = pa[other_rows, columns(j)].astype(BF)
        if j == 0:
            pl.semaphore_wait(barrier, len(peers))
        pair_copies.append(send(sta.at[:, columns(j)], rxa.at[:, columns(j)], pair))

    audio_count = alen[0]
    filled = alen[0] + tlen[0]
    me = slot(batch)
    mine = rows(me * HEAD, HEAD)
    theirs = rows(slot((1 - xhi) * 2 + c) * HEAD, HEAD)

    def square(i, acc):
        v = text[:, lanes_of(i, 128)].astype(F32)
        return acc + v * v

    squares = lax.fori_loop(0, width // 128, square, jnp.zeros((128, 128), F32))
    squares = jnp.broadcast_to(jnp.sum(squares, axis=1, keepdims=True), (128, 128))
    stat_out[...] = squares.T[:8]
    stat_copies = group(stat_in, [(stat_out, stat_in.at[k - 1], y_peers[k - 1]) for k in range(1, 4)])
    head_pos = lax.broadcasted_iota(jnp.int32, (HEAD, 1), 0)
    lane64 = lax.broadcasted_iota(jnp.int32, (HEAD, 128), 1)
    is_audio = head_pos < audio_count
    frm[mine, :] = jnp.where(
        jnp.logical_and(is_audio, lax.broadcasted_iota(jnp.int32, (HEAD, 512), 1) == 127), 1.0, 0.0
    ).astype(BF)
    for tap in range(4):
        block = taps[tap * HEAD : (tap + 1) * HEAD]
        frm[mine, tap * 128 : tap * 128 + feat] = jnp.where(is_audio, block, jnp.zeros_like(block))
    f_far = send(frm.at[mine], frm.at[mine], far)
    f_sib = send(frm.at[mine], frm.at[mine], sibling)
    gain_vals = gain[...].astype(F32)
    for i in range(width // 128):
        gains[0:1, i * 128 : (i + 1) * 128] = gain_vals[i : i + 1]
    gains[1:2, :] = 1.0 / gains[0:1, :]
    arrive(stat_copies)
    stat = stat_out[...] + stat_in[0] + stat_in[1] + stat_in[2]
    inv_text = lax.rsqrt(stat[0:1] / D + norm_eps)
    inv_text = jnp.broadcast_to(inv_text, (128, 128)).T
    totals[:, 0:128] = inv_text

    place = rows(c * 128 + x * 32, 32)
    pos = lax.broadcasted_iota(jnp.int32, (32, 1), 0) + 32 * xlo

    def gather_z(buf, j):
        own = buf.at[place, piece(j, z)]
        return group(buf.at[place, pl.ds(j * span, 7 * part)], [(own, own, p) for p in z_peers])

    def gather_x(buf, j):
        own = buf.at[place, columns(j)]
        right = send(own, own, x_peers[0])
        left = send(own, own, x_peers[2])
        direct = send(own, own, x_peers[1]) if j == CHUNKS - 1 else None
        return right, left, direct

    def hand_on(buf, j, right, left, direct):
        before = c * 128 + xmod(3) * 32
        after = c * 128 + xmod(1) * 32
        arrive(right)
        arrive(left)
        if direct is None:
            low = buf.at[rows(before, 16), columns(j)]
            high = buf.at[rows(after + 16, 16), columns(j)]
            both = buf.at[rows(c * 128 + xmod(2) * 32, 32), columns(j)]
            direct = group(both, [(low, low, x_peers[0]), (high, high, x_peers[2])])
        return direct

    def to_core(buf, j, direct):
        arrive(direct)
        half_rows = buf.at[rows(c * 128, 128), columns(j)]
        return send(half_rows, half_rows, sibling)

    def scatter_z(stage, landing, j):
        lanes = pl.ds(j * part, part)
        return group(
            landing.at[:, :, lanes],
            [(stage.at[:, piece(j, zmod(k))], landing.at[k - 1, :, lanes], z_peers[k - 1]) for k in range(1, 8)],
        )

    def pipeline(buf, order, first, second, last, extra):
        live = {}
        for t in range(CHUNKS + max(lag for _, lag in order)):
            for stage, lag in order:
                j = t - lag
                if j < 0 or j >= CHUNKS:
                    continue
                if stage == 0:
                    live[j] = first(j)
                elif stage == 1:
                    second(j, live[j])
                    live[j] = gather_z(buf, j)
                elif stage == 2:
                    arrive(live[j])
                    live[j] = gather_x(buf, j)
                elif stage == 3:
                    live[j] = hand_on(buf, j, *live[j])
                elif stage == 4:
                    live[j] = to_core(buf, j, live[j])
                else:
                    arrive(live[j])
                    last(j)
            extra(t)

    def pair_sum(j):
        arrive(pair_copies[j])
        out = pa[own_rows, columns(j)] + rxa[:, columns(j)].astype(F32)
        pa[own_rows, columns(j)] = out
        stz[:, columns(j)] = out.astype(stz.dtype)
        return scatter_z(stz, rza, j)

    def head_stream(j, copies):
        arrive(copies)
        lanes = piece(j, z)
        total = pa[own_rows, lanes]
        for k in range(7):
            total = total + rza[k, :, pl.ds(j * part, part)].astype(F32)
        words = text[own_rows, lanes].astype(F32) * totals[own_rows, 0:1]
        stream = jnp.where(pos < audio_count, total, jnp.where(pos < filled, words, 0.0))
        xh[place, lanes] = (stream * gains[0:1, lanes]).astype(BF)

    def project(buf, acc, j):
        lanes = columns(j)
        for start in range(0, PADDED, 256):
            size = min(256, PADDED - start)
            out = lax.dot_general(
                buf[:, lanes], w[pl.ds(start, size), lanes], (((1,), (1,)), ((), ())),
                preferred_element_type=F32,
            )
            if j == 0:
                acc[:, pl.ds(start, size)] = out
            else:
                acc[:, pl.ds(start, size)] += out

    def head_project(j):
        if j == 0:
            arrive_local()
            w[pl.ds(units, PADDED - units), :] = jnp.zeros((PADDED - units, width), BF)
            sqs[...] = jnp.zeros_like(sqs)

        def head_square(i, carry):
            lanes = lanes_of(j * (span // 128) + i, 128)
            v = xh[:, lanes].astype(F32) * gains[1:2, lanes]
            sqs[...] += v * v
            return carry

        lax.fori_loop(0, span // 128, head_square, 0)
        project(xh, gacc, j)

    def tail_tile(i):
        lanes = lanes_of(i, 512)
        vals = text[HEAD:, lanes].astype(F32) * totals[HEAD:, 0:1]
        xt[mine, lanes] = (jnp.where((head_pos + HEAD) < filled, vals, 0.0) * gains[0:1, lanes]).astype(BF)

    def during_head(t):
        if t == CHUNKS:
            tiles(width // 512, tail_tile)

    pipeline(xh, ((1, 2), (0, 0), (2, 3), (3, 4), (4, 5), (5, 6)), pair_sum, head_stream, head_project, during_head)
    lane256 = lax.broadcasted_iota(jnp.int32, (256, 128), 1)
    mark = units - (PADDED - 128)
    last_tile = pl.ds(PADDED - 128, 128)
    sq = jnp.sum(sqs[...], axis=1, keepdims=True)
    high = sq.astype(BF).astype(F32)
    gacc[:, last_tile] = jnp.where(
        lane256 == mark, high, jnp.where(lane256 == mark + 1, sq - high, gacc[:, last_tile])
    )

    def spread(acc, stage, base):
        stage[...] = acc[...].astype(BF)
        return group(
            grx.at[base : base + 3],
            [
                (stage.at[rows(slot(ymod(k)) * HEAD, HEAD)], grx.at[base + k - 1], y_peers[k - 1])
                for k in (2, 1, 3)
            ],
        )

    head_y = spread(gacc, gst, 0)
    cross_copy = send(xt.at[mine], xt.at[mine], cross)
    tail_sib = send(xt.at[mine], xt.at[mine], sibling)
    arrive(f_far)
    f_fwd = send(frm.at[theirs], frm.at[theirs], sibling)
    arrive(f_sib)
    arrive(f_fwd)
    arrive(head_y)

    keep = rows(slot(y) * HEAD, HEAD)

    def total_of(acc, base):
        t = acc[keep, :]
        for k in range(3):
            t = t + grx[base + k].astype(F32)
        return t

    totals[0:HEAD, :] = total_of(gacc, 0)
    totals[HEAD:, :] = jnp.zeros((128 - HEAD, PADDED), F32)
    flag = frm[keep, 0:128].astype(F32)[:, 127:128]
    totals[0:HEAD, last_tile] = jnp.where(lane64 == mark + 2, flag, totals[0:HEAD, last_tile])

    def activations():
        both = totals[...].T
        stat = both[units : units + 8]
        inv = jnp.where(stat[2:3] > 0.5, lax.rsqrt((stat[0:1] + stat[1:2]) / D + norm_eps), 1.0)
        gate = both[:half] * inv
        up = both[half:units] * inv
        sig = jax.nn.sigmoid(gate)
        return inv, gate, up, sig, gate * sig

    inv, gate, up, sig, silu = activations()
    cotv = cot[...].astype(F32)
    g_gate = cotv * up * sig * (1.0 + gate * (1.0 - sig))
    g_up = cotv * silu
    inner = jnp.sum(g_gate * gate + g_up * up, axis=0, keepdims=True) * (inv * inv) / D
    high = inner.astype(BF).astype(F32)
    row = lax.broadcasted_iota(jnp.int32, (PADDED - units, 128), 0)
    extra_rows = jnp.where(row == 0, high, jnp.where(row == 1, inner - high, 0.0))
    grads = jnp.concatenate([g_gate * inv, g_up * inv, extra_rows], axis=0).T
    gall[keep, :] = grads[:HEAD].astype(BF)
    g_copies = group(gall.at[0 : 3 * HEAD], [(gall.at[keep], gall.at[keep], p) for p in y_peers])
    frames_t = frm[...].T
    for tap in range(4):
        frames_out[tap * feat : (tap + 1) * feat] = frames_t[tap * 128 : tap * 128 + feat]
    arrive(g_copies)

    edge = gall[:, last_tile].astype(F32)
    marked = jnp.logical_or(lane256 == mark, lane256 == mark + 1)
    coefs[...] = jnp.broadcast_to(
        jnp.sum(jnp.where(marked, edge, 0.0), axis=1, keepdims=True), (256, 128)
    )

    def share(base, lanes):
        block = rows(base, 128)
        out = jnp.dot(gall[block, :], w[:, lanes], preferred_element_type=F32)
        unit = xh[block, lanes].astype(F32) * gains[1:2, lanes]
        return out * gains[0:1, lanes] - unit * coefs[block, 0:1]

    sib_copies, x_copies = {}, {}

    def to_sibling(j):
        def tile(i):
            lanes = lanes_of(j * (span // 512) + i, 512)
            bst[:, lanes] = share((1 - c) * 128, lanes)

        tiles(span // 512, tile)
        sib_copies[j] = send(bst.at[:, columns(j)], brx.at[:, columns(j)], sibling)

    def to_x(j):
        arrive(sib_copies[j])

        def tile(i):
            lanes = lanes_of(j * (span // 512) + i, 512)
            out = share(c * 128, lanes) + brx[:, lanes]
            xown[:, lanes] = out
            xst[:, lanes] = out.astype(BF)

        tiles(span // 512, tile)
        x_copies[j] = group(
            xrx.at[:, :, columns(j)],
            [
                (xst.at[rows(xmod(k) * 32, 32), columns(j)], xrx.at[k - 1, :, columns(j)], x_peers[k - 1])
                for k in (2, 1, 3)
            ],
        )

    to_sibling(0)
    for j in range(CHUNKS):
        if j + 1 < CHUNKS:
            to_sibling(j + 1)
        to_x(j)
    arrive(cross_copy)
    tail_fwd = send(xt.at[theirs], xt.at[theirs], sibling)
    mine32 = rows(x * 32, 32)

    def x_sum(j):
        arrive(x_copies[j])
        out = xown[mine32, columns(j)]
        for k in range(3):
            out = out + xrx[k, :, columns(j)].astype(F32)
        xown[mine32, columns(j)] = out
        zst[:, columns(j)] = out.astype(zst.dtype)
        return scatter_z(zst, zrx, j)

    def head_grad(j, copies):
        arrive(copies)
        lanes = piece(j, z)
        total = xown[mine32, lanes]
        for k in range(7):
            total = total + zrx[k, :, pl.ds(j * part, part)].astype(F32)
        grad_out[place, lanes] = total.astype(BF)

    tail_y = []

    def during_tail(t):
        if t < CHUNKS:
            if t == 0:
                arrive(tail_sib)
                arrive(tail_fwd)
            project(xt, tacc, t)
        if t == CHUNKS - 1:
            tail_y.append(spread(tacc, tst, 3))
        if t == CHUNKS + 2:
            arrive(tail_y[0])
            totals[HEAD:, :] = total_of(tacc, 3)
            _, _, up, _, silu = activations()
            hidden_out[...] = (silu * up).astype(BF)

    pipeline(grad_out, ((0, 0), (1, 1), (2, 2), (3, 3), (4, 4), (5, 5)), x_sum, head_grad, lambda j: None, during_tail)
    finish()


def weight_kernel(frames_t, grad, out):
    feat = out.shape[1]
    total = jnp.dot(frames_t[...], grad[...], preferred_element_type=F32)
    for tap in range(4):
        out[tap] = total[tap * feat : (tap + 1) * feat]


def on_device(
    frames, adapter_weight, text_embed, audio_len, text_len, norm_gain, gate_up, cotangent
):
    feat_here = frames.shape[2]
    width_here = adapter_weight.shape[2]
    units = 2 * gate_up.shape[2]
    depth = 4 * feat_here
    gain = norm_gain.reshape(width_here // 128, 128)
    weights = jnp.transpose(gate_up, (1, 2, 0)).reshape(units, width_here)
    cot = cotangent.T
    vmem = pl.BlockSpec(memory_space=pltpu.VMEM)
    smem = pl.BlockSpec(memory_space=pltpu.SMEM)
    scratch = [
        ((2, width_here), F32),
        ((PADDED, width_here), BF),
        ((256, width_here), BF),
        ((256, width_here), BF),
        ((4 * HEAD, feat_here), BF),
        ((256, 512), BF),
        ((HEAD, width_here), F32),
        ((32, width_here), BF),
        ((32, width_here), BF),
        ((32, width_here), SUMS_A),
        ((7, 32, width_here // 8), SUMS_A),
        ((8, 128), F32),
        ((3, 8, 128), F32),
        ((256, PADDED), F32),
        ((256, PADDED), F32),
        ((256, 128), F32),
        ((256, PADDED), BF),
        ((256, PADDED), BF),
        ((6, HEAD, PADDED), BF),
        ((128, PADDED), F32),
        ((256, PADDED), BF),
        ((256, 128), F32),
        ((128, width_here), F32),
        ((128, width_here), F32),
        ((128, width_here), BF),
        ((128, width_here), F32),
        ((3, 32, width_here), BF),
        ((32, width_here), SUMS_B),
        ((7, 32, width_here // 8), SUMS_B),
    ]
    hidden, grad, frames_t = pl.pallas_call(
        fused_kernel,
        out_shape=(
            jax.ShapeDtypeStruct((units // 2, 128), BF),
            jax.ShapeDtypeStruct((256, width_here), BF),
            jax.ShapeDtypeStruct((depth, 256), BF),
        ),
        in_specs=[smem, smem] + [vmem] * 5 + [pl.BlockSpec(memory_space=pl.ANY)],
        out_specs=(vmem, vmem, vmem),
        scratch_shapes=[pltpu.VMEM(s, t) for s, t in scratch]
        + [
            pltpu.SemaphoreType.DMA((COPIES,)),
            pltpu.SemaphoreType.DMA((COPIES,)),
            pltpu.SemaphoreType.DMA,
        ],
        compiler_params=pltpu.CompilerParams(
            collective_id=0, has_side_effects=True, vmem_limit_bytes=56 << 20
        ),
    )(audio_len, text_len, frames[0].T, adapter_weight, text_embed, gain, cot, weights)
    tile = width_here // 4
    weight_grad = pl.pallas_call(
        weight_kernel,
        grid=(width_here // tile,),
        out_shape=jax.ShapeDtypeStruct((4, feat_here, width_here), F32),
        in_specs=[
            pl.BlockSpec((depth, 256), lambda i: (0, 0)),
            pl.BlockSpec((256, tile), lambda i: (0, i)),
        ],
        out_specs=pl.BlockSpec((4, feat_here, tile), lambda i: (0, 0, i)),
    )(frames_t, grad)
    return (hidden.T, weight_grad)


def solution(mesh):
    return jax.shard_map(
        on_device,
        mesh=mesh,
        in_specs=(
            P("batch", None, "hidden"),
            P(None, "hidden", "width"),
            P("batch", "width"),
            P("batch"),
            P("batch"),
            P("width"),
            P("width", None, ("batch", "hidden")),
            P("width", ("batch", "hidden")),
        ),
        out_specs=(P("width", ("batch", "hidden")), P(None, "hidden", "width")),
        check_vma=False,
    )
```
